1024 devices in a mesh: grp: 128 (over z, y_hi, core), tm: 8 (over x, y_lo).
Axes of the slice: x: 4, y: 8 (y_hi: 4, y_lo: 2; y = y_hi * 2 + y_lo), z: 16, core: 2. Of those that a mesh axis runs over, the one named last changes fastest.
Arguments:
- features: bfloat16 [512, 2048, 1024], P('grp', 'tm'), may hold values from -40 to 40
- frame_counts: int32 [512], P('grp'), may hold values from 512 to 2048
- pool_query: bfloat16 [8, 1024], replicated, may hold values from -4 to 4
- w_proj: bfloat16 [1024, 512], replicated, may hold values from -0.1875 to 0.1875
- doc_embed: bfloat16 [16384, 512], P(('grp', 'tm')), may hold values from -0.25 to 0.25
- doc_index: int32 [512], replicated, may hold values from 0 to 16383
Outputs:
- loss: float32 [512], P('grp')
- speech_grad: float32 [512, 512], P('grp')
- doc_grad: float32 [16384, 512], P(('grp', 'tm'))
The draws below stay inside these ranges and needn't reach their ends.
All inputs are finite; a program needn't handle non-finite values.
Results may differ from the reference program's by a relative error of at most 0.0044.
Values may be sent and summed in bfloat16 or wider, within the bound.
A program may use at most 32 MiB of HBM per device.

```python
import math
import jax
import jax.numpy as jnp
from jax import lax

C = 1024
E = 512
H = 8
RECS = 512
FRAMES = 2048
DOCS = 16384


def shared_query(key):
    return jnp.clip(jax.random.normal(jax.random.fold_in(key, 11), (H, C), jnp.float32), -4.0, 4.0)


def draw_pool_query(key, part):
    return shared_query(key).astype(jnp.bfloat16)


def draw_features(key, part):
    noise_key = jax.random.fold_in(key, 12)
    return jnp.clip(jax.random.normal(noise_key, (RECS, FRAMES, C), jnp.float32), -6.0, 6.0).astype(jnp.bfloat16)


def plant(drawn, key, least, top_value):
    shape = drawn.shape
    index_at = [jax.random.randint(jax.random.fold_in(key, axis), (), 0, shape[axis]) for axis in range(len(shape))]
    drawn = drawn.at[tuple(index_at)].set(least)
    longest = shape.index(max(shape))
    index_at[longest] = (index_at[longest] + 1) % shape[longest]
    return drawn.at[tuple(index_at)].set(top_value)


def steps_of(key, extent, shards, low, high):
    gain, own = 1.0, jax.random.fold_in(key, 6)
    for position, shards_of in shards:
        steps = jnp.exp(jax.random.uniform(jax.random.fold_in(own, position), (shards_of,), jnp.float32, low / len(shards), high / len(shards)))
        gain = gain * jnp.repeat(steps, extent[position] // shards_of).reshape([-1 if axis == position else 1 for axis in range(len(extent))])
    return gain


def scatter_about(stream_key, extent, deviation, reach, pieces=(), kind=jnp.bfloat16):
    values = deviation * jax.random.normal(stream_key, extent, jnp.float32)
    if pieces:
        values = values * steps_of(stream_key, extent, pieces, -0.22, 0.18)
    return jnp.clip(values, -reach, reach).astype(kind)


def setup_inputs(seed: int = 0) -> dict:
    seeds = jax.random.split(jax.random.key(seed), 7)
    return {
        "features": draw_features(jax.random.fold_in(seeds[6], 71), 0),
        "frame_counts": plant(jax.random.randint(seeds[1], (RECS,), FRAMES // 4, FRAMES + 1), jax.random.fold_in(seeds[1], 1), FRAMES // 4, FRAMES).astype(jnp.int32),
        "pool_query": draw_pool_query(jax.random.fold_in(seeds[6], 71), 0),
        "w_proj": scatter_about(seeds[3], (C, E), C ** -0.5, 0.1875),
        "doc_embed": scatter_about(seeds[4], (DOCS, E), E ** -0.5, 0.25, ((0, 1024),)),
        "doc_index": plant(jax.random.randint(seeds[5], (RECS,), 0, DOCS), jax.random.fold_in(seeds[5], 1), 0, DOCS - 1).astype(jnp.int32),
    }


logit_scale = 10.0
logit_shift = -8.0
norm_eps = 1e-06

def reference(features, frame_counts, pool_query, w_proj, doc_embed, doc_index):

    def pool_one(inputs):
        frames, count = inputs
        values = jnp.dot(frames, w_proj, preferred_element_type=jnp.float32).astype(jnp.bfloat16)
        scores = jnp.dot(pool_query, frames.T, preferred_element_type=jnp.float32) / math.sqrt(C)
        valid = (jnp.arange(FRAMES, dtype=jnp.int32) < count)[None, :]
        masked = jnp.where(valid, scores, -1e+30)
        peak_score = lax.optimization_barrier(jnp.max(masked, axis=1))
        weights = jnp.where(valid, jnp.exp(masked - peak_score[:, None]), 0.0)
        totals = lax.optimization_barrier(jnp.sum(weights, axis=1))
        weights_b = weights.astype(jnp.bfloat16).astype(jnp.float32)
        head_values = values.astype(jnp.float32).reshape(FRAMES, H, E // H)
        numerator = jnp.einsum('hf,fhd->hd', weights_b, head_values)
        return (numerator / totals[:, None]).reshape(E)
    pooled = lax.map(pool_one, (features, frame_counts))
    speech = (pooled * lax.rsqrt(lax.optimization_barrier(jnp.sum(pooled * pooled, axis=1, keepdims=True)) + norm_eps)).astype(jnp.bfloat16)
    logits = logit_scale * jnp.dot(speech, doc_embed.T, preferred_element_type=jnp.float32) + logit_shift
    doc_ids = jnp.arange(DOCS, dtype=jnp.int32)
    labels = jnp.where(doc_index[:, None] == doc_ids[None, :], 1.0, -1.0)
    loss = lax.optimization_barrier(jnp.sum(jax.nn.softplus(-labels * logits), axis=1))
    grad_b = (-labels * jax.nn.sigmoid(-labels * logits)).astype(jnp.bfloat16)
    speech_grad = logit_scale * jnp.dot(grad_b, doc_embed, preferred_element_type=jnp.float32)
    doc_grad = logit_scale * jnp.dot(grad_b.T, speech, preferred_element_type=jnp.float32)
    return (loss, speech_grad, doc_grad)
```

```python
import math

import jax
import jax.numpy as jnp
from jax import lax
from jax.sharding import PartitionSpec as P

logit_scale = 10.0
logit_shift = -8.0
norm_eps = 1e-06


def pair_tile(speech_rows, rec_start, doc_rows, doc_start, doc_index):
    row_count = speech_rows.shape[0]
    logits = (
        logit_scale * jnp.dot(speech_rows, doc_rows.T, preferred_element_type=jnp.float32)
        + logit_shift
    )
    targets = lax.dynamic_slice_in_dim(doc_index, rec_start, row_count)
    doc_ids = doc_start + jnp.arange(doc_rows.shape[0], dtype=jnp.int32)
    labels = jnp.where(targets[:, None] == doc_ids[None, :], 1.0, -1.0)
    losses = jnp.sum(jax.nn.softplus(-labels * logits), axis=1)
    grad_b = (-labels * jax.nn.sigmoid(-labels * logits)).astype(jnp.bfloat16)
    speech_part = logit_scale * jnp.dot(grad_b, doc_rows, preferred_element_type=jnp.float32)
    doc_part = logit_scale * jnp.dot(grad_b.T, speech_rows, preferred_element_type=jnp.float32)
    return (losses, speech_part, doc_part)


def body(features, frame_counts, pool_query, w_proj, doc_embed, doc_index):
    rec_count, frame_dev, channels = features.shape
    width = w_proj.shape[1]
    heads = pool_query.shape[0]
    doc_dev = doc_embed.shape[0]
    values = jnp.dot(
        features.reshape(rec_count * frame_dev, channels),
        w_proj,
        preferred_element_type=jnp.float32,
    ).astype(jnp.bfloat16)
    values = values.reshape(rec_count, frame_dev, heads, width // heads)
    scores = jnp.einsum(
        "rfc,hc->rhf", features, pool_query, preferred_element_type=jnp.float32
    ) / math.sqrt(channels)
    positions = lax.axis_index("tm") * frame_dev + jnp.arange(frame_dev, dtype=jnp.int32)
    valid = (positions[None, :] < frame_counts[:, None])[:, None, :]
    masked = jnp.where(valid, scores, -1e30)
    peak_score = lax.pmax(jnp.max(masked, axis=2), "tm")
    weights = jnp.where(valid, jnp.exp(masked - peak_score[:, :, None]), 0.0)
    totals = jnp.sum(weights, axis=2)
    numerator = jnp.einsum(
        "rhf,rfhd->rhd", weights.astype(jnp.bfloat16), values, preferred_element_type=jnp.float32
    )
    numerator, totals = lax.psum((numerator, totals), "tm")
    pooled = (numerator / totals[:, :, None]).reshape(rec_count, width)
    speech = (
        pooled * lax.rsqrt(jnp.sum(pooled * pooled, axis=1, keepdims=True) + norm_eps)
    ).astype(jnp.bfloat16)
    doc_start = (lax.axis_index("grp") * lax.axis_size("tm") + lax.axis_index("tm")) * doc_dev
    all_speech = lax.all_gather(speech, "grp", axis=0, tiled=True)
    losses, speech_part, doc_grad = pair_tile(all_speech, 0, doc_embed, doc_start, doc_index)
    loss_rows = jnp.broadcast_to(losses[:, None], (losses.shape[0], 128))
    packed = jnp.concatenate([speech_part, loss_rows], axis=1)
    packed = lax.psum_scatter(packed, "grp", scatter_dimension=0, tiled=True)
    packed = lax.psum(packed, "tm")
    return (packed[:, width], packed[:, :width], doc_grad)


def solution(mesh):
    placed = (P("grp", "tm", None), P("grp"), P(), P(), P(("grp", "tm"), None), P())
    return jax.shard_map(
        body,
        mesh=mesh,
        in_specs=placed,
        out_specs=(P("grp"), P("grp", None), P(("grp", "tm"), None)),
        check_vma=False,
    )
```

```python
import functools
import math

import jax
import jax.numpy as jnp
from jax import lax
from jax.experimental import pallas as pl
from jax.experimental.pallas import tpu as pltpu
from jax.sharding import PartitionSpec as P

logit_scale = 10.0
logit_shift = -8.0
norm_eps = 1e-06
lowest = -1e30

y_hi = 4
cores = 2
lanes = 128


def each(count, step):
    def run(index, carry):
        step(index)
        return carry

    lax.fori_loop(0, count, run, 0)


def iota(shape, axis):
    return lax.broadcasted_iota(jnp.int32, shape, axis)


def dot(a, b, contract_b=0):
    return lax.dot_general(
        a, b, (((1,), (contract_b,)), ((), ())), preferred_element_type=jnp.float32
    )


def kernel(
    rings,
    columns,
    counts_ref,
    index_ref,
    feat_ref,
    query_ref,
    proj_ref,
    docs_ref,
    loss_ref,
    speech_grad_ref,
    doc_grad_ref,
    feat,
    proj,
    docs,
    part_out,
    part_in,
    speech_in,
    target,
    grad_out,
    grad_in,
    total_out,
    total_in,
    doc_out,
    doc_in,
    load_sem,
    docs_sems,
    part_sems,
    speech_sems,
    grad_sems,
    total_sems,
    doc_sems,
):
    recs, frames, channels = feat_ref.shape
    width = proj_ref.shape[1]
    heads = query_ref.shape[0]
    head_width = width // heads
    doc_dev = docs_ref.shape[0]
    halves = columns // y_hi
    pair = recs // halves
    chunks = width // lanes
    rows = rings * 8
    team = columns * cores

    group = lax.axis_index("grp")
    column = lax.axis_index("tm")
    core = lax.rem(group, cores)
    row_y = lax.rem(lax.div(group, cores), y_hi)
    ring = lax.div(group, cores * y_hi)
    me = column * cores + core
    half = lax.rem(lax.div(column, 2), 2)
    served = lax.div(column, 4) * 2 + lax.rem(column, 2)

    def group_of(z, y, c):
        return (z * y_hi + y) * cores + c

    def column_of(y, part):
        return (lax.div(y, 2) * 2 + part) * 2 + lax.rem(y, 2)

    is_server = served == row_y

    def team_peer(step):
        other = lax.rem(me + step + 1, team)
        return other, (group_of(ring, row_y, lax.rem(other, cores)), lax.div(other, cores))

    def ring_peer(step):
        other = lax.rem(ring + step + 1, rings)
        return other, (group_of(other, row_y, core), column)

    def server_peer(step):
        y, part = lax.div(step, halves), lax.rem(step, halves)
        place = column_of(row_y, part)
        return part, (y == row_y) & (place == column), (group_of(ring, y, core), place)

    def client_peer(step):
        return is_server & (step == column), (group_of(ring, served, core), step)

    def remote(source, target_ref, sems, send, receive, device):
        return pltpu.make_async_remote_copy(
            src_ref=source,
            dst_ref=target_ref,
            send_sem=sems.at[0, send],
            recv_sem=sems.at[1, receive],
            device_id=device,
            device_id_type=pl.DeviceIdType.MESH,
        )

    def arrival(buffer, sems, slot):
        pltpu.make_async_copy(buffer.at[slot], buffer.at[slot], sems.at[1, slot]).wait()

    loads = [
        pltpu.make_async_copy(feat_ref.at[rec], feat.at[rec], load_sem.at[rec])
        for rec in range(recs)
    ]
    loads.append(pltpu.make_async_copy(proj_ref, proj, load_sem.at[recs]))
    for load in loads:
        load.start()

    barrier = pltpu.get_barrier_semaphore()

    def greet(device):
        pl.semaphore_signal(
            barrier, inc=1, device_id=device, device_id_type=pl.DeviceIdType.MESH
        )

    each(team - 1, lambda step: greet(team_peer(step)[1]))
    each(rings - 1, lambda step: greet(ring_peer(step)[1]))

    def greet_server(step):
        _, own, device = server_peer(step)

        @pl.when(jnp.logical_not(own))
        def _():
            greet(device)

    def greet_client(step):
        own, device = client_peer(step)

        @pl.when(jnp.logical_not(own))
        def _():
            greet(device)

    each(y_hi * halves, greet_server)
    each(columns, greet_client)

    first_rec = group_of(0, served, core) * recs + half * pair
    odd = (iota((8, lanes), 0) & 1) == 1

    def fill_target(z):
        at = first_rec + z * (y_hi * cores * recs)
        target[pl.ds(pl.multiple_of(z * 8, 8), 8), :] = jnp.where(
            odd, index_ref[at + 1], index_ref[at]
        )

    each(rings, fill_target)
    docs[me] = docs_ref[...]

    lane_head = lax.shift_right_logical(iota((heads, width), 1), int(math.log2(head_width)))
    own_head = lane_head == iota((heads, width), 0)
    position = column * frames + iota((heads, frames), 1)

    def pool(rec):
        loads[rec].wait()
        block = feat[rec]
        scores = dot(query_ref[...], block, 1) / math.sqrt(channels)
        valid = position < counts_ref[rec]
        masked = jnp.where(valid, scores, lowest)
        peak = jnp.max(masked, axis=1, keepdims=True)
        weights = jnp.where(valid, jnp.exp(masked - peak), 0.0)
        total = jnp.sum(weights, axis=1, keepdims=True)
        some = total > 0.0
        safe = jnp.where(some, total, 1.0)
        mean = dot(weights.astype(jnp.bfloat16), block) / safe
        return mean, jnp.where(some, peak + jnp.log(safe), lowest)

    pooled = [pool(0)]

    expected = team - 1 + rings - 1 + y_hi * halves + columns
    pl.semaphore_wait(barrier, expected - jnp.where(is_server, 2, 0))

    def docs_copy(step):
        other, device = team_peer(step)
        return remote(docs.at[me], docs.at[me], docs_sems, other, me, device)

    each(team - 1, lambda step: docs_copy(step).start())

    for rec in range(1, recs):
        pooled.append(pool(rec))
    means = jnp.concatenate([mean for mean, _ in pooled], axis=0)
    high = means.astype(jnp.bfloat16)
    low = (means - high.astype(jnp.float32)).astype(jnp.bfloat16)
    loads[recs].wait()
    projected = dot(jnp.concatenate([high, low], axis=0), proj[...])
    projected = projected[: recs * heads] + projected[recs * heads :]
    for rec in range(recs):
        own = projected[rec * heads : (rec + 1) * heads]
        row = jnp.sum(jnp.where(own_head, own, 0.0), axis=0, keepdims=True)
        level = jnp.sum(jnp.where(own_head, pooled[rec][1], 0.0), axis=0, keepdims=True)
        part, place = rec // pair, rec % pair
        for chunk in range(chunks):
            at = chunk * pair + place
            span = slice(chunk * lanes, (chunk + 1) * lanes)
            part_out[part, at : at + 1, :] = row[:, span]
            part_out[part, 8 + at : 9 + at, :] = level[:, span]

    def part_copy(step):
        part, own, device = server_peer(step)
        return own, part, remote(
            part_out.at[part], part_in.at[column], part_sems, step, column, device
        )

    def part_start(step):
        own, part, copy = part_copy(step)

        @pl.when(jnp.logical_not(own))
        def _():
            copy.start()

        @pl.when(own)
        def _():
            pltpu.make_async_copy(
                part_out.at[part], part_in.at[column], part_sems.at[1, column]
            ).start()

    each(y_hi * halves, part_start)
    each(columns, lambda slot: arrival(part_in, part_sems, slot))

    parts = part_in[...]
    levels = parts[:, 8:, :]
    shares = jnp.exp(levels - jnp.max(levels, axis=0, keepdims=True))
    mean = jnp.sum(shares * parts[:, :8, :], axis=0) / jnp.sum(shares, axis=0)
    squares = mean * mean
    scale_even = lax.rsqrt(jnp.sum(jnp.where(odd, 0.0, squares), keepdims=True) + norm_eps)
    scale_odd = lax.rsqrt(jnp.sum(jnp.where(odd, squares, 0.0), keepdims=True) + norm_eps)
    speech_in[ring] = (mean * jnp.where(odd, scale_odd, scale_even)).astype(jnp.bfloat16)

    def speech_copy(step):
        other, device = ring_peer(step)
        return remote(
            speech_in.at[ring], speech_in.at[ring], speech_sems, other, ring, device
        )

    each(rings - 1, lambda step: speech_copy(step).start())

    def from_others(count, own, buffer, sems):
        each(count - 1, lambda step: arrival(buffer, sems, lax.rem(own + step + 1, count)))

    from_others(team, me, docs, docs_sems)
    from_others(rings, ring, speech_in, speech_sems)

    pieces = speech_in[...].astype(jnp.float32).reshape(rows, lanes).astype(jnp.bfloat16)
    row_at, col_at = iota((rows, rows), 0), iota((rows, rows), 1)
    whole = []
    for chunk in range(chunks):
        pick = col_at == (row_at & -8) + chunk * pair + (row_at & 1)
        pick = jnp.where(pick, 1.0, 0.0).astype(jnp.bfloat16)
        whole.append(dot(pick, pieces).astype(jnp.bfloat16))
    speech = jnp.concatenate(whole, axis=1)
    all_docs = docs[...].reshape(team * doc_dev, width)
    logits = logit_scale * dot(speech, all_docs, 1) + logit_shift

    lane = iota((1, team * doc_dev), 1)
    slot = lax.div(lane, doc_dev)
    doc_group = group_of(ring, row_y, lax.rem(slot, cores))
    doc_id = (doc_group * columns + lax.div(slot, cores)) * doc_dev + lax.rem(lane, doc_dev)
    hit = target[:, :1] == doc_id
    signed = jnp.where(hit, -logits, logits)
    tail = jnp.exp(-jnp.abs(signed))
    losses = jnp.sum(
        jnp.maximum(signed, 0.0) + jnp.log1p(tail), axis=1, keepdims=True
    )
    chance = jnp.where(signed >= 0.0, 1.0, tail) / (1.0 + tail)
    grad = jnp.where(hit, -chance, chance)
    grad_b = grad.astype(jnp.bfloat16)

    chunk_row = lax.shift_right_logical(iota((rows, lanes), 0) & 7, 1)
    wide = dot(grad_b, all_docs)
    picked = jnp.zeros((rows, lanes), jnp.float32)
    for chunk in range(chunks):
        span = slice(chunk * lanes, (chunk + 1) * lanes)
        picked = jnp.where(chunk_row == chunk, wide[:, span], picked)
    loss_high = losses.astype(jnp.bfloat16).astype(jnp.float32)
    loss_low = losses - loss_high
    loss_rows = jnp.where(chunk_row == 0, loss_high, jnp.where(chunk_row == 1, loss_low, 0.0))
    message = jnp.concatenate(
        [picked.reshape(rings, 8, lanes), loss_rows.reshape(rings, 8, lanes)], axis=1
    )
    grad_out[...] = message.astype(jnp.bfloat16)
    grad_in[ring] = grad_out[ring]

    def grad_copy(step):
        other, device = ring_peer(step)
        return remote(grad_out.at[other], grad_in.at[ring], grad_sems, other, ring, device)

    each(rings - 1, lambda step: grad_copy(step).start())

    first_chunk = lax.shift_right_logical(iota((rows, team * doc_dev), 0) & 7, 1) == 0
    once = jnp.where(first_chunk, grad, 0.0).T.astype(jnp.bfloat16)
    doc_part = dot(once, speech).astype(jnp.bfloat16)
    doc_out[...] = doc_part.reshape(team, doc_dev, width)
    doc_in[me] = doc_out[me]

    def doc_copy(step):
        other, device = team_peer(step)
        return remote(doc_out.at[other], doc_in.at[me], doc_sems, other, me, device)

    each(team - 1, lambda step: doc_copy(step).start())

    from_others(rings, ring, grad_in, grad_sems)
    total_out[...] = jnp.sum(grad_in[...].astype(jnp.float32), axis=0)
    place = row_y * halves + half

    def total_copy(step):
        own, device = client_peer(step)
        return own, remote(total_out, total_in.at[place], total_sems, step, place, device)

    def total_start(step):
        own, copy = total_copy(step)

        @pl.when(jnp.logical_not(own))
        def _():
            copy.start()

        @pl.when(own)
        def _():
            pltpu.make_async_copy(
                total_out, total_in.at[place], total_sems.at[1, place]
            ).start()

    each(columns, total_start)

    from_others(team, me, doc_in, doc_sems)
    doc_grad_ref[...] = jnp.sum(doc_in[...].astype(jnp.float32), axis=0)

    each(y_hi * halves, lambda slot: arrival(total_in, total_sems, slot))
    for part in range(halves):
        total = total_in[part]
        for y in range(1, y_hi):
            total += total_in[y * halves + part]
        for place_in in range(pair):
            rec = part * pair + place_in
            for chunk in range(chunks):
                at = chunk * pair + place_in
                speech_grad_ref[rec : rec + 1, chunk * lanes : (chunk + 1) * lanes] = total[
                    at : at + 1
                ]
            high_at, low_at = 8 + place_in, 8 + pair + place_in
            loss_ref[rec : rec + 1, :] = total[high_at : high_at + 1] + total[low_at : low_at + 1]

    each(team - 1, lambda step: docs_copy(step).wait_send())
    each(rings - 1, lambda step: speech_copy(step).wait_send())
    each(rings - 1, lambda step: grad_copy(step).wait_send())
    each(team - 1, lambda step: doc_copy(step).wait_send())

    def part_end(step):
        own, _, copy = part_copy(step)

        @pl.when(jnp.logical_not(own))
        def _():
            copy.wait_send()

    def total_end(step):
        own, copy = total_copy(step)

        @pl.when(jnp.logical_not(own))
        def _():
            copy.wait_send()

    each(y_hi * halves, part_end)
    each(columns, total_end)


def body(groups, columns, features, frame_counts, pool_query, w_proj, doc_embed, doc_index):
    recs, frames, channels = features.shape
    width = w_proj.shape[1]
    doc_dev = doc_embed.shape[0]
    rings = groups // (y_hi * cores)
    halves = columns // y_hi
    team = columns * cores
    smem = pl.BlockSpec(memory_space=pltpu.SMEM)
    vmem = pl.BlockSpec(memory_space=pltpu.VMEM)
    anywhere = pl.BlockSpec(memory_space=pl.ANY)
    f32, bf16 = jnp.float32, jnp.bfloat16
    sems = pltpu.SemaphoreType.DMA
    loss, speech_grad, doc_grad = pl.pallas_call(
        functools.partial(kernel, rings, columns),
        out_shape=(
            jax.ShapeDtypeStruct((recs, lanes), f32),
            jax.ShapeDtypeStruct((recs, width), f32),
            jax.ShapeDtypeStruct((doc_dev, width), f32),
        ),
        in_specs=[smem, smem, anywhere, vmem, anywhere, vmem],
        out_specs=(vmem, vmem, vmem),
        scratch_shapes=[
            pltpu.VMEM((recs, frames, channels), bf16),
            pltpu.VMEM((channels, width), bf16),
            pltpu.VMEM((team, doc_dev, width), bf16),
            pltpu.VMEM((halves, 16, lanes), f32),
            pltpu.VMEM((columns, 16, lanes), f32),
            pltpu.VMEM((rings, 8, lanes), bf16),
            pltpu.VMEM((rings * 8, lanes), jnp.int32),
            pltpu.VMEM((rings, 16, lanes), bf16),
            pltpu.VMEM((rings, 16, lanes), bf16),
            pltpu.VMEM((16, lanes), f32),
            pltpu.VMEM((y_hi * halves, 16, lanes), f32),
            pltpu.VMEM((team, doc_dev, width), bf16),
            pltpu.VMEM((team, doc_dev, width), bf16),
            sems((recs + 1,)),
            sems((2, team)),
            sems((2, max(columns, y_hi * halves))),
            sems((2, rings)),
            sems((2, rings)),
            sems((2, max(columns, y_hi * halves))),
            sems((2, team)),
        ],
        compiler_params=pltpu.CompilerParams(
            collective_id=0, has_side_effects=True, vmem_limit_bytes=32 * 2**20
        ),
    )(frame_counts, doc_index, features, pool_query, w_proj, doc_embed)
    return (loss[:, 0], logit_scale * speech_grad, logit_scale * doc_grad)


def solution(mesh):
    placed = (P("grp", "tm", None), P("grp"), P(), P(), P(("grp", "tm"), None), P())
    return jax.shard_map(
        functools.partial(body, mesh.shape["grp"], mesh.shape["tm"]),
        mesh=mesh,
        in_specs=placed,
        out_specs=(P("grp"), P("grp", None), P(("grp", "tm"), None)),
        check_vma=False,
    )
```

```python
import functools
import math

import jax
import jax.numpy as jnp
from jax import lax
from jax.experimental import pallas as pl
from jax.experimental.pallas import tpu as pltpu
from jax.sharding import PartitionSpec as P

logit_scale = 10.0
logit_shift = -8.0
norm_eps = 1e-06
lowest = -1e30

y_hi = 4
cores = 2
lanes = 128


def each(count, step):
    def run(index, carry):
        step(index)
        return carry

    lax.fori_loop(0, count, run, 0)


def bits(count):
    return count.bit_length() - 1


def iota(shape, axis):
    return lax.broadcasted_iota(jnp.int32, shape, axis)


def dot(a, b, contract_b=0):
    return lax.dot_general(
        a, b, (((1,), (contract_b,)), ((), ())), preferred_element_type=jnp.float32
    )


def kernel(
    rings,
    columns,
    counts_ref,
    index_ref,
    feat_ref,
    query_ref,
    proj_ref,
    docs_ref,
    loss_ref,
    speech_grad_ref,
    doc_grad_ref,
    counts,
    index,
    feat,
    query,
    proj,
    docs,
    part_out,
    part_in,
    speech_in,
    target,
    grad_out,
    grad_in,
    total_out,
    total_in,
    doc_out,
    doc_in,
    load_sem,
    docs_sems,
    part_sems,
    speech_sems,
    grad_sems,
    total_sems,
    doc_sems,
):
    recs, frames, channels = feat_ref.shape
    width = proj_ref.shape[1]
    heads = query_ref.shape[0]
    head_width = width // heads
    doc_dev = docs_ref.shape[0]
    halves = columns // y_hi
    pair = recs // halves
    chunks = width // lanes
    rows = rings * 8
    team = columns * cores
    servers = y_hi * halves

    group = lax.axis_index("grp")
    column = lax.axis_index("tm")
    core = group & 1
    row_y = (group >> 1) & (y_hi - 1)
    ring = group >> bits(cores * y_hi)
    me = column * cores + core
    half = (column >> 1) & 1
    served = (column >> 2) * 2 + (column & 1)

    def group_of(z, y, c):
        return (z * y_hi + y) * cores + c

    def column_of(y, part):
        return ((y >> 1) * 2 + part) * 2 + (y & 1)

    is_server = served == row_y

    def team_peer(step):
        other = me ^ (step + 1)
        return other, (group_of(ring, row_y, other & 1), other >> 1)

    def ring_peer(step):
        off = (step + 1) >> 1
        other = (ring + rings // 2 + jnp.where((step & 1) == 1, -off, off)) & (rings - 1)
        return other, (group_of(other, row_y, core), column)

    def server_peer(step):
        y, part = step >> 1, step & 1
        place = column_of(row_y, part)
        return part, (y == row_y) & (place == column), (group_of(ring, y, core), place)

    def client_peer(step):
        return is_server & (step == column), (group_of(ring, served, core), step)

    def remote(source, target_ref, sems, send, receive, device):
        return pltpu.make_async_remote_copy(
            src_ref=source,
            dst_ref=target_ref,
            send_sem=sems.at[0, send],
            recv_sem=sems.at[1, receive],
            device_id=device,
            device_id_type=pl.DeviceIdType.MESH,
        )

    def arrival(buffer, sems, slot):
        pltpu.make_async_copy(buffer.at[slot], buffer.at[slot], sems.at[1, slot]).wait()

    def from_others(count, own, buffer, sems):
        each(count - 1, lambda step: arrival(buffer, sems, own ^ (step + 1)))

    def docs_copy(step):
        other, device = team_peer(step)
        return remote(docs.at[me], docs.at[me], docs_sems, other, me, device)

    def part_copy(step):
        part, own, device = server_peer(step)
        return own, part, remote(
            part_out.at[part], part_in.at[column], part_sems, step, column, device
        )

    def speech_copy(step):
        other, device = ring_peer(step)
        return remote(
            speech_in.at[ring], speech_in.at[ring], speech_sems, other, ring, device
        )

    def grad_copy(step):
        other, device = ring_peer(step)
        return remote(grad_out.at[other], grad_in.at[ring], grad_sems, other, ring, device)

    def doc_copy(step):
        other, device = team_peer(step)
        return remote(doc_out.at[other], doc_in.at[me], doc_sems, other, me, device)

    place_out = row_y * halves + half

    def total_copy(step):
        own, device = client_peer(step)
        return own, remote(
            total_out, total_in.at[place_out], total_sems, step, place_out, device
        )

    loads = [
        pltpu.make_async_copy(source, buffer, load_sem.at[number])
        for number, (source, buffer) in enumerate(
            [
                (feat_ref, feat),
                (query_ref, query),
                (counts_ref, counts),
                (proj_ref, proj),
                (docs_ref, docs.at[me]),
                (index_ref, index),
            ]
        )
    ]
    barrier = pltpu.get_barrier_semaphore()

    def greet(device):
        pl.semaphore_signal(
            barrier, inc=1, device_id=device, device_id_type=pl.DeviceIdType.MESH
        )

    def greet_server(step):
        _, own, device = server_peer(step)

        @pl.when(jnp.logical_not(own))
        def _():
            greet(device)

    def greet_client(step):
        own, device = client_peer(step)

        @pl.when(jnp.logical_not(own))
        def _():
            greet(device)

    def enter():
        for load in loads:
            load.start()
        each(servers, greet_server)
        each(columns, greet_client)
        each(rings - 1, lambda step: greet(ring_peer(step)[1]))
        each(team - 1, lambda step: greet(team_peer(step)[1]))

    def pool():
        for load in loads[:3]:
            load.wait()
        every = feat[...].reshape(recs * frames, channels)
        all_scores = dot(query[...], every, 1) / math.sqrt(channels)
        position = column * frames + iota((heads, frames), 1)
        lane_head = iota((heads, width), 1) >> bits(head_width)
        own_head = lane_head == iota((heads, width), 0)
        means, levels = [], []
        for rec in range(recs):
            scores = all_scores[:, rec * frames : (rec + 1) * frames]
            valid = position < counts[rec]
            masked = jnp.where(valid, scores, lowest)
            peak = jnp.max(masked, axis=1, keepdims=True)
            weights = jnp.where(valid, jnp.exp(masked - peak), 0.0)
            total = jnp.sum(weights, axis=1, keepdims=True)
            some = total > 0.0
            safe = jnp.where(some, total, 1.0)
            means.append(dot(weights.astype(jnp.bfloat16), feat[rec]) / safe)
            levels.append(jnp.where(some, peak + jnp.log(safe), lowest))
        means = jnp.concatenate(means, axis=0)
        high = means.astype(jnp.bfloat16)
        low = (means - high.astype(jnp.float32)).astype(jnp.bfloat16)
        loads[3].wait()
        projected = dot(jnp.concatenate([high, low], axis=0), proj[...])
        projected = projected[: recs * heads] + projected[recs * heads :]
        for rec in range(recs):
            own = projected[rec * heads : (rec + 1) * heads]
            row = jnp.sum(jnp.where(own_head, own, 0.0), axis=0, keepdims=True)
            level = jnp.sum(jnp.where(own_head, levels[rec], 0.0), axis=0, keepdims=True)
            part, place = rec // pair, rec % pair
            for chunk in range(chunks):
                at = chunk * pair + place
                span = slice(chunk * lanes, (chunk + 1) * lanes)
                part_out[part, at : at + 1, :] = row[:, span]
                part_out[part, 8 + at : 9 + at, :] = level[:, span]

    def meet():
        expected = team - 1 + rings - 1 + servers + columns
        pl.semaphore_wait(barrier, expected - jnp.where(is_server, 2, 0))

    def send_parts():
        def start(step):
            own, part, copy = part_copy(step)

            @pl.when(jnp.logical_not(own))
            def _():
                copy.start()

            @pl.when(own)
            def _():
                pltpu.make_async_copy(
                    part_out.at[part], part_in.at[column], part_sems.at[1, column]
                ).start()

        each(servers, start)

    def send_docs():
        loads[4].wait()
        each(team - 1, lambda step: docs_copy(step).start())
        loads[5].wait()
        first_rec = group_of(0, served, core) * recs + half * pair
        odd = (iota((8, lanes), 0) & 1) == 1

        def fill_target(z):
            at = first_rec + z * (y_hi * cores * recs)
            target[pl.ds(pl.multiple_of(z * 8, 8), 8), :] = jnp.where(
                odd, index[at + 1], index[at]
            )

        each(rings, fill_target)

    def merge_parts():
        each(columns, lambda slot: arrival(part_in, part_sems, slot))
        odd = (iota((8, lanes), 0) & 1) == 1
        parts = part_in[...]
        levels = parts[:, 8:, :]
        shares = jnp.exp(levels - jnp.max(levels, axis=0, keepdims=True))
        mean = jnp.sum(shares * parts[:, :8, :], axis=0) / jnp.sum(shares, axis=0)
        squares = mean * mean
        even_sum = jnp.sum(jnp.where(odd, 0.0, squares), keepdims=True)
        odd_sum = jnp.sum(jnp.where(odd, squares, 0.0), keepdims=True)
        scale = lax.rsqrt(jnp.where(odd, odd_sum, even_sum) + norm_eps)
        speech_in[ring] = (mean * scale).astype(jnp.bfloat16)

    def send_speech():
        each(rings - 1, lambda step: speech_copy(step).start())

    def await_speech():
        from_others(team, me, docs, docs_sems)
        from_others(rings, ring, speech_in, speech_sems)

    def score():
        pieces = speech_in[...].astype(jnp.float32).reshape(rows, lanes).astype(jnp.bfloat16)
        row_at, col_at = iota((rows, rows), 0), iota((rows, rows), 1)
        whole = []
        for chunk in range(chunks):
            pick = col_at == (row_at & -8) + chunk * pair + (row_at & 1)
            pick = jnp.where(pick, 1.0, 0.0).astype(jnp.bfloat16)
            whole.append(dot(pick, pieces).astype(jnp.bfloat16))
        speech = jnp.concatenate(whole, axis=1)
        all_docs = docs[...].reshape(team * doc_dev, width)
        logits = logit_scale * dot(speech, all_docs, 1) + logit_shift

        lane = iota((1, team * doc_dev), 1)
        slot = lane >> bits(doc_dev)
        doc_group = group_of(ring, row_y, slot & 1)
        doc_id = (doc_group * columns + (slot >> 1)) * doc_dev + (lane & (doc_dev - 1))
        hit = target[:, :1] == doc_id
        signed = jnp.where(hit, -logits, logits)
        tail = jnp.exp(-jnp.abs(signed))
        losses = jnp.sum(
            jnp.maximum(signed, 0.0) + jnp.log1p(tail), axis=1, keepdims=True
        )
        chance = jnp.where(signed >= 0.0, 1.0, tail) / (1.0 + tail)
        grad = jnp.where(hit, -chance, chance)
        grad_b = grad.astype(jnp.bfloat16)

        chunk_row = (iota((rows, lanes), 0) & 7) >> 1
        wide = dot(grad_b, all_docs)
        picked = jnp.zeros((rows, lanes), jnp.float32)
        for chunk in range(chunks):
            span = slice(chunk * lanes, (chunk + 1) * lanes)
            picked = jnp.where(chunk_row == chunk, wide[:, span], picked)
        loss_high = losses.astype(jnp.bfloat16).astype(jnp.float32)
        loss_low = losses - loss_high
        loss_rows = jnp.where(chunk_row == 0, loss_high, jnp.where(chunk_row == 1, loss_low, 0.0))
        message = jnp.concatenate(
            [picked.reshape(rings, 8, lanes), loss_rows.reshape(rings, 8, lanes)], axis=1
        )
        grad_out[...] = message.astype(jnp.bfloat16)
        grad_in[ring] = grad_out[ring]
        each(rings - 1, lambda step: grad_copy(step).start())

        first_chunk = (iota((rows, team * doc_dev), 0) & 7) >> 1 == 0
        once = jnp.where(first_chunk, grad, 0.0).T.astype(jnp.bfloat16)
        doc_part = dot(once, speech).astype(jnp.bfloat16)
        doc_out[...] = doc_part.reshape(team, doc_dev, width)
        doc_in[me] = doc_out[me]
        each(team - 1, lambda step: doc_copy(step).start())

    def sum_grads():
        from_others(rings, ring, grad_in, grad_sems)
        total_out[...] = jnp.sum(grad_in[...].astype(jnp.float32), axis=0)

        def start(step):
            own, copy = total_copy(step)

            @pl.when(jnp.logical_not(own))
            def _():
                copy.start()

            @pl.when(own)
            def _():
                pltpu.make_async_copy(
                    total_out, total_in.at[place_out], total_sems.at[1, place_out]
                ).start()

        each(columns, start)

    def sum_docs():
        from_others(team, me, doc_in, doc_sems)
        doc_grad_ref[...] = jnp.sum(doc_in[...].astype(jnp.float32), axis=0)

    def sum_totals():
        each(servers, lambda slot: arrival(total_in, total_sems, slot))
        for part in range(halves):
            total = total_in[part]
            for y in range(1, y_hi):
                total += total_in[y * halves + part]
            for place in range(pair):
                rec = part * pair + place
                for chunk in range(chunks):
                    at = chunk * pair + place
                    span = slice(chunk * lanes, (chunk + 1) * lanes)
                    speech_grad_ref[rec : rec + 1, span] = total[at : at + 1]
                high, low = 8 + place, 8 + pair + place
                loss_ref[rec : rec + 1, :] = total[high : high + 1] + total[low : low + 1]

    def drain():
        def part_end(step):
            own, _, copy = part_copy(step)

            @pl.when(jnp.logical_not(own))
            def _():
                copy.wait_send()

        def total_end(step):
            own, copy = total_copy(step)

            @pl.when(jnp.logical_not(own))
            def _():
                copy.wait_send()

        each(servers, part_end)
        each(team - 1, lambda step: docs_copy(step).wait_send())
        each(rings - 1, lambda step: speech_copy(step).wait_send())
        each(rings - 1, lambda step: grad_copy(step).wait_send())
        each(team - 1, lambda step: doc_copy(step).wait_send())
        each(columns, total_end)

    enter()
    pool()
    meet()
    send_parts()
    send_docs()
    merge_parts()
    send_speech()
    await_speech()
    score()
    sum_grads()
    sum_docs()
    sum_totals()
    drain()


def body(groups, columns, features, frame_counts, pool_query, w_proj, doc_embed, doc_index):
    recs, frames, channels = features.shape
    width = w_proj.shape[1]
    doc_dev = doc_embed.shape[0]
    rings = groups // (y_hi * cores)
    halves = columns // y_hi
    team = columns * cores
    vmem = pl.BlockSpec(memory_space=pltpu.VMEM)
    anywhere = pl.BlockSpec(memory_space=pl.ANY)
    f32, bf16 = jnp.float32, jnp.bfloat16
    sems = pltpu.SemaphoreType.DMA
    loss, speech_grad, doc_grad = pl.pallas_call(
        functools.partial(kernel, rings, columns),
        out_shape=(
            jax.ShapeDtypeStruct((recs, lanes), f32),
            jax.ShapeDtypeStruct((recs, width), f32),
            jax.ShapeDtypeStruct((doc_dev, width), f32),
        ),
        in_specs=[anywhere] * 6,
        out_specs=(vmem, vmem, vmem),
        scratch_shapes=[
            pltpu.SMEM(frame_counts.shape, jnp.int32),
            pltpu.SMEM(doc_index.shape, jnp.int32),
            pltpu.VMEM((recs, frames, channels), bf16),
            pltpu.VMEM(pool_query.shape, bf16),
            pltpu.VMEM((channels, width), bf16),
            pltpu.VMEM((team, doc_dev, width), bf16),
            pltpu.VMEM((halves, 16, lanes), f32),
            pltpu.VMEM((columns, 16, lanes), f32),
            pltpu.VMEM((rings, 8, lanes), bf16),
            pltpu.VMEM((rings * 8, lanes), jnp.int32),
            pltpu.VMEM((rings, 16, lanes), bf16),
            pltpu.VMEM((rings, 16, lanes), bf16),
            pltpu.VMEM((16, lanes), f32),
            pltpu.VMEM((y_hi * halves, 16, lanes), f32),
            pltpu.VMEM((team, doc_dev, width), bf16),
            pltpu.VMEM((team, doc_dev, width), bf16),
            sems((6,)),
            sems((2, team)),
            sems((2, max(columns, y_hi * halves))),
            sems((2, rings)),
            sems((2, rings)),
            sems((2, max(columns, y_hi * halves))),
            sems((2, team)),
        ],
        compiler_params=pltpu.CompilerParams(collective_id=0, has_side_effects=True),
    )(frame_counts, doc_index, features, pool_query, w_proj, doc_embed)
    return (loss[:, 0], logit_scale * speech_grad, logit_scale * doc_grad)


def solution(mesh):
    placed = (P("grp", "tm", None), P("grp"), P(), P(), P(("grp", "tm"), None), P())
    return jax.shard_map(
        functools.partial(body, mesh.shape["grp"], mesh.shape["tm"]),
        mesh=mesh,
        in_specs=placed,
        out_specs=(P("grp"), P("grp", None), P(("grp", "tm"), None)),
        check_vma=False,
    )
```

```python
import functools
import math

import jax
import jax.numpy as jnp
from jax import lax
from jax.experimental import pallas as pl
from jax.experimental.pallas import tpu as pltpu
from jax.sharding import PartitionSpec as P

logit_scale = 10.0
logit_shift = -8.0
norm_eps = 1e-06
lowest = -1e30

team = 8
lanes = 128


def each(count, step):
    def run(index, carry):
        step(index)
        return carry

    lax.fori_loop(0, count, run, 0)


def bits(count):
    return count.bit_length() - 1


def iota(shape, axis):
    return lax.broadcasted_iota(jnp.int32, shape, axis)


def dot(a, b, contract_b=0):
    return lax.dot_general(
        a, b, (((1,), (contract_b,)), ((), ())), preferred_element_type=jnp.float32
    )


def selector(hit):
    return jnp.where(hit, 1.0, 0.0).astype(jnp.bfloat16)


def kernel(
    rings,
    columns,
    counts_ref,
    index_ref,
    feat_ref,
    query_ref,
    proj_ref,
    docs_ref,
    loss_ref,
    speech_grad_ref,
    doc_grad_ref,
    counts,
    index,
    feat,
    query,
    proj,
    docs,
    part_out,
    part_in,
    speech_in,
    target,
    grad_out,
    grad_in,
    total_out,
    total_in,
    doc_out,
    doc_in,
    load_sem,
    docs_sems,
    part_sems,
    speech_sems,
    grad_sems,
    total_sems,
    doc_sems,
):
    recs, frames, channels = feat_ref.shape
    width = proj_ref.shape[1]
    heads = query_ref.shape[0]
    head_width = width // heads
    doc_dev = docs_ref.shape[0]
    chunks = width // lanes
    packed = chunks * recs

    group = lax.axis_index("grp")
    column = lax.axis_index("tm")
    ring = group >> bits(team)
    member = group & (team - 1)

    def ring_peer(step):
        off = (step + 1) >> 1
        other = (ring + rings // 2 + jnp.where((step & 1) == 1, -off, off)) & (rings - 1)
        return other, (other * team + member, column)

    def team_peer(step):
        other = member ^ (step + 1)
        return other, (ring * team + other, column)

    def column_peer(step):
        other = column ^ (step + 1)
        return other, (group, other)

    class Exchange:
        def __init__(self, count, own, peer, source, buffer, sems, same):
            self.count, self.own, self.peer = count, own, peer
            self.source, self.buffer, self.sems, self.same = source, buffer, sems, same

        def copy(self, step):
            other, device = self.peer(step)
            return pltpu.make_async_remote_copy(
                src_ref=self.source if self.same else self.source.at[other],
                dst_ref=self.buffer.at[self.own],
                send_sem=self.sems.at[0, other],
                recv_sem=self.sems.at[1, self.own],
                device_id=device,
                device_id_type=pl.DeviceIdType.MESH,
            )

        def send(self):
            each(self.count - 1, lambda step: self.copy(step).start())

        def receive(self):
            def arrival(step):
                block = self.buffer.at[self.own ^ (step + 1)]
                pltpu.make_async_copy(
                    block, block, self.sems.at[1, self.own ^ (step + 1)]
                ).wait()

            each(self.count - 1, arrival)

        def drain(self):
            each(self.count - 1, lambda step: self.copy(step).wait_send())

    along_ring = functools.partial(Exchange, rings, ring, ring_peer)
    in_team = functools.partial(Exchange, team, member, team_peer)
    in_column = functools.partial(Exchange, columns, column, column_peer)
    docs_move = in_team(docs.at[member], docs, docs_sems, True)
    part_move = in_column(part_out, part_in, part_sems, True)
    speech_move = along_ring(speech_in.at[ring], speech_in, speech_sems, True)
    grad_move = along_ring(grad_out, grad_in, grad_sems, False)
    total_move = in_column(total_out, total_in, total_sems, True)
    doc_move = in_team(doc_out, doc_in, doc_sems, False)

    loads = [
        pltpu.make_async_copy(source, buffer, load_sem.at[number])
        for number, (source, buffer) in enumerate(
            [
                (feat_ref, feat),
                (query_ref, query),
                (counts_ref, counts),
                (proj_ref, proj),
                (docs_ref, docs.at[member]),
                (index_ref, index),
            ]
        )
    ]
    barrier = pltpu.get_barrier_semaphore()

    def greet(device):
        pl.semaphore_signal(
            barrier, inc=1, device_id=device, device_id_type=pl.DeviceIdType.MESH
        )

    def enter():
        for load in loads:
            load.start()
        each(rings - 1, lambda step: greet(ring_peer(step)[1]))
        each(team - 1, lambda step: greet(team_peer(step)[1]))
        each(columns - 1, lambda step: greet(column_peer(step)[1]))

    def pool():
        for load in loads[:3]:
            load.wait()
        every = feat[...].reshape(recs * frames, channels)
        all_scores = dot(query[...], every, 1) / math.sqrt(channels)
        position = column * frames + iota((heads, frames), 1)
        lane_head = iota((heads, width), 1) >> bits(head_width)
        own_head = lane_head == iota((heads, width), 0)
        means, levels = [], []
        for rec in range(recs):
            scores = all_scores[:, rec * frames : (rec + 1) * frames]
            valid = position < counts[rec]
            masked = jnp.where(valid, scores, lowest)
            peak = jnp.max(masked, axis=1, keepdims=True)
            weights = jnp.where(valid, jnp.exp(masked - peak), 0.0)
            total = jnp.sum(weights, axis=1, keepdims=True)
            some = total > 0.0
            safe = jnp.where(some, total, 1.0)
            means.append(dot(weights.astype(jnp.bfloat16), feat[rec]) / safe)
            levels.append(jnp.where(some, peak + jnp.log(safe), lowest))
        means = jnp.concatenate(means, axis=0)
        high = means.astype(jnp.bfloat16)
        low = (means - high.astype(jnp.float32)).astype(jnp.bfloat16)
        loads[3].wait()
        projected = dot(jnp.concatenate([high, low], axis=0), proj[...])
        projected = projected[: recs * heads] + projected[recs * heads :]
        for rec in range(recs):
            own = projected[rec * heads : (rec + 1) * heads]
            row = jnp.sum(jnp.where(own_head, own, 0.0), axis=0, keepdims=True)
            level = jnp.sum(jnp.where(own_head, levels[rec], 0.0), axis=0, keepdims=True)
            for chunk in range(chunks):
                at = chunk * recs + rec
                span = slice(chunk * lanes, (chunk + 1) * lanes)
                part_out[at : at + 1, :] = row[:, span]
                part_out[packed + at : packed + at + 1, :] = level[:, span]

    def meet():
        pl.semaphore_wait(barrier, rings - 1 + team - 1 + columns - 1)

    def send_parts():
        part_move.send()
        part_in[column] = part_out[...]

    def send_docs():
        loads[4].wait()
        docs_move.send()
        loads[5].wait()
        row = iota((8, lanes), 0)

        def fill(block):
            value = jnp.zeros((8, lanes), jnp.int32)
            for j in range(8):
                place = block * (8 // recs) + j // recs
                number = (place * team + member) * recs + j % recs
                value = jnp.where(row == j, index[number], value)
            target[pl.ds(pl.multiple_of(block * 8, 8), 8), :] = value

        each(rings * recs // 8, fill)

    def merge_parts():
        part_move.receive()
        parts = part_in[...]
        levels = parts[:, packed:, :]
        shares = jnp.exp(levels - jnp.max(levels, axis=0, keepdims=True))
        mean = jnp.sum(shares * parts[:, :packed, :], axis=0) / jnp.sum(shares, axis=0)
        squares = jnp.sum(mean * mean, axis=1, keepdims=True)
        rec_at = iota((packed, 1), 0) & (recs - 1)
        sums = jnp.zeros((packed, 1), jnp.float32)
        for rec in range(recs):
            mine = rec_at == rec
            sums = jnp.where(
                mine, jnp.sum(jnp.where(mine, squares, 0.0), axis=0, keepdims=True), sums
            )
        speech_in[ring] = (mean * lax.rsqrt(sums + norm_eps)).astype(jnp.bfloat16)
        speech_move.send()

    def score():
        docs_move.receive()
        speech_move.receive()
        pieces = speech_in[...].reshape(rings * packed, lanes)
        shape = (rings * recs, rings * packed)
        row, col = iota(shape, 0), iota(shape, 1)
        base = (row >> bits(recs)) * packed + (row & (recs - 1))
        whole = [
            dot(selector(col == base + chunk * recs), pieces).astype(jnp.bfloat16)
            for chunk in range(chunks)
        ]
        speech = jnp.concatenate(whole, axis=1)
        all_docs = docs[...].reshape(team * doc_dev, width)
        logits = logit_scale * dot(speech, all_docs, 1) + logit_shift
        lane = iota((1, team * doc_dev), 1)
        device = (ring * team + (lane >> bits(doc_dev))) * columns + column
        hit = target[:, :1] == device * doc_dev + (lane & (doc_dev - 1))
        signed = jnp.where(hit, -logits, logits)
        tail = jnp.exp(-jnp.abs(signed))
        losses = jnp.sum(jnp.maximum(signed, 0.0) + jnp.log1p(tail), axis=1, keepdims=True)
        chance = jnp.where(signed >= 0.0, 1.0, tail) / (1.0 + tail)
        grad = jnp.where(hit, -chance, chance)

        shape = (rings * packed, rings * recs)
        row, col = iota(shape, 0), iota(shape, 1)
        spread = selector(col == (row >> bits(packed)) * recs + (row & (recs - 1)))
        wide = dot(dot(spread, grad.astype(jnp.bfloat16)).astype(jnp.bfloat16), all_docs)
        chunk_at = (iota((rings * packed, lanes), 0) & (packed - 1)) >> bits(recs)
        picked = wide[:, :lanes]
        for chunk in range(1, chunks):
            span = slice(chunk * lanes, (chunk + 1) * lanes)
            picked = jnp.where(chunk_at == chunk, wide[:, span], picked)

        shape = (rings * 8, rings * recs)
        row, col = iota(shape, 0), iota(shape, 1)
        spread = selector(col == (row >> 3) * recs + (row & (recs - 1)))
        high = jnp.broadcast_to(losses.astype(jnp.bfloat16), (rings * recs, lanes))
        low = (losses - high.astype(jnp.float32)).astype(jnp.bfloat16)
        is_high = (iota((rings * 8, lanes), 0) & 7) < recs
        loss_rows = jnp.where(is_high, dot(spread, high), dot(spread, low))
        message = jnp.concatenate(
            [picked.reshape(rings, packed, lanes), loss_rows.reshape(rings, 8, lanes)], axis=1
        )
        grad_out[...] = message.astype(jnp.bfloat16)
        grad_move.send()
        grad_in[ring] = grad_out[ring]

        doc_part = dot(grad.T.astype(jnp.bfloat16), speech).astype(jnp.bfloat16)
        doc_out[...] = doc_part.reshape(team, doc_dev, width)
        doc_move.send()
        doc_in[member] = doc_out[member]

    def sum_grads():
        grad_move.receive()
        total = jnp.sum(grad_in[...].astype(jnp.float32), axis=0)
        total_out[...] = total
        total_move.send()
        total_in[column] = total

    def sum_docs():
        doc_move.receive()
        doc_grad_ref[...] = logit_scale * jnp.sum(doc_in[...].astype(jnp.float32), axis=0)

    def sum_totals():
        total_move.receive()
        total = jnp.sum(total_in[...], axis=0)
        for chunk in range(chunks):
            span = slice(chunk * lanes, (chunk + 1) * lanes)
            speech_grad_ref[:, span] = logit_scale * total[chunk * recs : (chunk + 1) * recs]
        loss_ref[...] = total[packed : packed + recs] + total[packed + recs : packed + 2 * recs]

    def drain():
        for move in (
            part_move,
            docs_move,
            speech_move,
            grad_move,
            doc_move,
            total_move,
        ):
            move.drain()

    enter()
    pool()
    meet()
    send_parts()
    send_docs()
    merge_parts()
    score()
    sum_grads()
    sum_docs()
    sum_totals()
    drain()


def finish(loss_ref, speech_grad_ref, doc_grad_ref, loss_out, speech_grad_out, doc_grad_out):
    speech_grad_out[...] = speech_grad_ref[...]
    doc_grad_out[...] = doc_grad_ref[...]
    shape = loss_ref.shape
    own = iota(shape, 0) == iota(shape, 1)
    loss_out[...] = jnp.sum(jnp.where(own, loss_ref[...], 0.0), axis=0)[: shape[0]]


def body(groups, columns, features, frame_counts, pool_query, w_proj, doc_embed, doc_index):
    recs, frames, channels = features.shape
    width = w_proj.shape[1]
    doc_dev = doc_embed.shape[0]
    rings = groups // team
    packed = width // lanes * recs
    vmem = pl.BlockSpec(memory_space=pltpu.VMEM)
    f32, bf16, i32 = jnp.float32, jnp.bfloat16, jnp.int32
    sems = pltpu.SemaphoreType.DMA
    loss, speech_grad, doc_grad = pl.pallas_call(
        functools.partial(kernel, rings, columns),
        out_shape=(
            jax.ShapeDtypeStruct((recs, lanes), f32),
            jax.ShapeDtypeStruct((recs, width), f32),
            jax.ShapeDtypeStruct((doc_dev, width), f32),
        ),
        in_specs=[pl.BlockSpec(memory_space=pltpu.MemorySpace.HBM)] * 6,
        out_specs=(vmem, vmem, vmem),
        scratch_shapes=[
            pltpu.SMEM(frame_counts.shape, i32),
            pltpu.SMEM(doc_index.shape, i32),
            pltpu.VMEM(features.shape, bf16),
            pltpu.VMEM(pool_query.shape, bf16),
            pltpu.VMEM(w_proj.shape, bf16),
            pltpu.VMEM((team, doc_dev, width), bf16),
            pltpu.VMEM((2 * packed, lanes), f32),
            pltpu.VMEM((columns, 2 * packed, lanes), f32),
            pltpu.VMEM((rings, packed, lanes), bf16),
            pltpu.VMEM((rings * recs, lanes), i32),
            pltpu.VMEM((rings, packed + 8, lanes), bf16),
            pltpu.VMEM((rings, packed + 8, lanes), bf16),
            pltpu.VMEM((packed + 8, lanes), f32),
            pltpu.VMEM((columns, packed + 8, lanes), f32),
            pltpu.VMEM((team, doc_dev, width), bf16),
            pltpu.VMEM((team, doc_dev, width), bf16),
            sems((6,)),
            sems((2, team)),
            sems((2, columns)),
            sems((2, rings)),
            sems((2, rings)),
            sems((2, columns)),
            sems((2, team)),
        ],
        compiler_params=pltpu.CompilerParams(
            collective_id=0, has_side_effects=True, vmem_limit_bytes=16 * 2**20
        ),
    )(
        *(
            pltpu.with_memory_space_constraint(array, pltpu.MemorySpace.HBM)
            for array in (frame_counts, doc_index, features, pool_query, w_proj, doc_embed)
        )
    )
    return pl.pallas_call(
        finish,
        out_shape=(
            jax.ShapeDtypeStruct((recs,), f32),
            jax.ShapeDtypeStruct((recs, width), f32),
            jax.ShapeDtypeStruct((doc_dev, width), f32),
        ),
        in_specs=[vmem] * 3,
        out_specs=(vmem, vmem, vmem),
        compiler_params=pltpu.CompilerParams(vmem_limit_bytes=16 * 2**20),
    )(loss, speech_grad, doc_grad)


def solution(mesh):
    placed = (P("grp", "tm", None), P("grp"), P(), P(), P(("grp", "tm"), None), P())
    return jax.shard_map(
        functools.partial(body, mesh.shape["grp"], mesh.shape["tm"]),
        mesh=mesh,
        in_specs=placed,
        out_specs=(P("grp"), P("grp", None), P(("grp", "tm"), None)),
        check_vma=False,
    )
```

```python
import functools
import math

import jax
import jax.numpy as jnp
from jax import lax
from jax.experimental import pallas as pl
from jax.experimental.pallas import tpu as pltpu
from jax.sharding import PartitionSpec as P

logit_scale = 10.0
logit_shift = -8.0
norm_eps = 1e-06
lowest = -1e30

team = 8
lanes = 128


def each(count, step):
    def run(index, carry):
        step(index)
        return carry

    lax.fori_loop(0, count, run, 0)


def bits(count):
    return count.bit_length() - 1


def iota(shape, axis):
    return lax.broadcasted_iota(jnp.int32, shape, axis)


def dot(a, b, contract_b=0):
    return lax.dot_general(
        a, b, (((1,), (contract_b,)), ((), ())), preferred_element_type=jnp.float32
    )


def selector(hit):
    return jnp.where(hit, 1.0, 0.0).astype(jnp.bfloat16)


def kernel(
    rings,
    columns,
    counts_ref,
    index_ref,
    feat_ref,
    query_ref,
    proj_ref,
    docs_ref,
    loss_ref,
    speech_grad_ref,
    doc_grad_ref,
    counts,
    index,
    feat,
    query,
    proj,
    docs,
    part_out,
    part_in,
    speech_in,
    target,
    grad_out,
    grad_in,
    total_out,
    total_in,
    doc_out,
    doc_in,
    load_sem,
    docs_sems,
    part_sems,
    speech_sems,
    grad_sems,
    total_sems,
    doc_sems,
    column_sem,
    ring_sem,
):
    recs, frames, channels = feat_ref.shape
    width = proj_ref.shape[1]
    heads = query_ref.shape[0]
    head_width = width // heads
    doc_dev = docs_ref.shape[0]
    chunks = width // lanes
    packed = chunks * recs

    group = lax.axis_index("grp")
    column = lax.axis_index("tm")
    ring = group >> bits(team)
    member = group & (team - 1)

    def ring_peer(step):
        off = (step + 1) >> 1
        other = (ring + rings // 2 + jnp.where((step & 1) == 1, -off, off)) & (rings - 1)
        return other, (other * team + member, column)

    def team_peer(step):
        other = member ^ (step + 1)
        return other, (ring * team + other, column)

    def column_peer(step):
        other = column ^ (step + 1)
        return other, (group, other)

    class Exchange:
        def __init__(self, count, own, peer, source, buffer, sems, same):
            self.count, self.own, self.peer = count, own, peer
            self.source, self.buffer, self.sems, self.same = source, buffer, sems, same

        def copy(self, step):
            other, device = self.peer(step)
            return pltpu.make_async_remote_copy(
                src_ref=self.source if self.same else self.source.at[other],
                dst_ref=self.buffer.at[self.own],
                send_sem=self.sems.at[0, other],
                recv_sem=self.sems.at[1, self.own],
                device_id=device,
                device_id_type=pl.DeviceIdType.MESH,
            )

        def send(self):
            each(self.count - 1, lambda step: self.copy(step).start())

        def receive(self):
            def arrival(step):
                block = self.buffer.at[self.own ^ (step + 1)]
                pltpu.make_async_copy(
                    block, block, self.sems.at[1, self.own ^ (step + 1)]
                ).wait()

            each(self.count - 1, arrival)

        def drain(self):
            each(self.count - 1, lambda step: self.copy(step).wait_send())

    along_ring = functools.partial(Exchange, rings, ring, ring_peer)
    in_team = functools.partial(Exchange, team, member, team_peer)
    in_column = functools.partial(Exchange, columns, column, column_peer)
    docs_move = in_team(docs.at[member], docs, docs_sems, True)
    part_move = in_column(part_out, part_in, part_sems, True)
    speech_move = along_ring(speech_in.at[ring], speech_in, speech_sems, True)
    grad_move = along_ring(grad_out, grad_in, grad_sems, False)
    total_move = in_column(total_out, total_in, total_sems, True)
    doc_move = in_team(doc_out, doc_in, doc_sems, False)

    loads = [
        pltpu.make_async_copy(source, buffer, load_sem.at[number])
        for number, (source, buffer) in enumerate(
            [
                (feat_ref, feat),
                (query_ref, query),
                (counts_ref, counts),
                (proj_ref, proj),
                (docs_ref, docs.at[member]),
                (index_ref, index),
            ]
        )
    ]
    barrier = pltpu.get_barrier_semaphore()

    def greet(device):
        pl.semaphore_signal(
            barrier, inc=1, device_id=device, device_id_type=pl.DeviceIdType.MESH
        )

    def enter():
        for load in loads:
            load.start()
        even = column - (column & 1)
        each(rings - 1, lambda step: greet((ring_peer(step)[1][0], even)))
        each(team - 1, lambda step: greet((team_peer(step)[1][0], even)))

        def greet_odd(step):
            @pl.when(step * 2 + 1 != column)
            def _():
                greet((group, step * 2 + 1))

        each(columns // 2, greet_odd)

    def pool():
        for load in loads[:3]:
            load.wait()
        every = feat[...].reshape(recs * frames, channels)
        all_scores = dot(query[...], every, 1) / math.sqrt(channels)
        position = column * frames + iota((heads, frames), 1)
        lane_head = iota((heads, width), 1) >> bits(head_width)
        own_head = lane_head == iota((heads, width), 0)
        means, levels = [], []
        for rec in range(recs):
            scores = all_scores[:, rec * frames : (rec + 1) * frames]
            valid = position < counts[rec]
            masked = jnp.where(valid, scores, lowest)
            peak = jnp.max(masked, axis=1, keepdims=True)
            weights = jnp.where(valid, jnp.exp(masked - peak), 0.0)
            total = jnp.sum(weights, axis=1, keepdims=True)
            some = total > 0.0
            safe = jnp.where(some, total, 1.0)
            means.append(dot(weights.astype(jnp.bfloat16), feat[rec]) / safe)
            levels.append(jnp.where(some, peak + jnp.log(safe), lowest))
        means = jnp.concatenate(means, axis=0)
        high = means.astype(jnp.bfloat16)
        low = (means - high.astype(jnp.float32)).astype(jnp.bfloat16)
        loads[3].wait()
        projected = dot(jnp.concatenate([high, low], axis=0), proj[...])
        projected = projected[: recs * heads] + projected[recs * heads :]
        for rec in range(recs):
            own = projected[rec * heads : (rec + 1) * heads]
            row = jnp.sum(jnp.where(own_head, own, 0.0), axis=0, keepdims=True)
            level = jnp.sum(jnp.where(own_head, levels[rec], 0.0), axis=0, keepdims=True)
            for chunk in range(chunks):
                at = chunk * recs + rec
                span = slice(chunk * lanes, (chunk + 1) * lanes)
                part_out[at : at + 1, :] = row[:, span]
                part_out[packed + at : packed + at + 1, :] = level[:, span]

    is_odd = (column & 1) == 1

    def tell_partner(sem):
        pl.semaphore_signal(
            sem, inc=1, device_id=(group, column ^ 1), device_id_type=pl.DeviceIdType.MESH
        )

    def meet_column():
        @pl.when(is_odd)
        def _():
            pl.semaphore_wait(barrier, columns - 1)
            tell_partner(column_sem)

        @pl.when(jnp.logical_not(is_odd))
        def _():
            pl.semaphore_wait(column_sem, 1)

    def open_ring():
        @pl.when(jnp.logical_not(is_odd))
        def _():
            pl.semaphore_wait(barrier, 2 * (rings - 1 + team - 1))
            tell_partner(ring_sem)

    def meet_ring():
        @pl.when(is_odd)
        def _():
            pl.semaphore_wait(ring_sem, 1)

    def send_parts():
        part_move.send()
        part_in[column] = part_out[...]

    def send_docs():
        loads[4].wait()
        docs_move.send()

    def fill_targets():
        loads[5].wait()
        row = iota((8, lanes), 0)

        def fill(block):
            value = jnp.zeros((8, lanes), jnp.int32)
            for j in range(8):
                place = block * (8 // recs) + j // recs
                number = (place * team + member) * recs + j % recs
                value = jnp.where(row == j, index[number], value)
            target[pl.ds(pl.multiple_of(block * 8, 8), 8), :] = value

        each(rings * recs // 8, fill)

    def merge_parts():
        part_move.receive()
        parts = part_in[...]
        levels = parts[:, packed:, :]
        shares = jnp.exp(levels - jnp.max(levels, axis=0, keepdims=True))
        mean = jnp.sum(shares * parts[:, :packed, :], axis=0) / jnp.sum(shares, axis=0)
        squares = jnp.sum(mean * mean, axis=1, keepdims=True)
        rec_at = iota((packed, 1), 0) & (recs - 1)
        sums = jnp.zeros((packed, 1), jnp.float32)
        for rec in range(recs):
            mine = rec_at == rec
            sums = jnp.where(
                mine, jnp.sum(jnp.where(mine, squares, 0.0), axis=0, keepdims=True), sums
            )
        speech_in[ring] = (mean * lax.rsqrt(sums + norm_eps)).astype(jnp.bfloat16)

    def score():
        docs_move.receive()
        speech_move.receive()
        pieces = speech_in[...].reshape(rings * packed, lanes)
        shape = (rings * recs, rings * packed)
        row, col = iota(shape, 0), iota(shape, 1)
        base = (row >> bits(recs)) * packed + (row & (recs - 1))
        whole = [
            dot(selector(col == base + chunk * recs), pieces).astype(jnp.bfloat16)
            for chunk in range(chunks)
        ]
        speech = jnp.concatenate(whole, axis=1)
        all_docs = docs[...].reshape(team * doc_dev, width)
        logits = logit_scale * dot(speech, all_docs, 1) + logit_shift
        lane = iota((1, team * doc_dev), 1)
        device = (ring * team + (lane >> bits(doc_dev))) * columns + column
        hit = target[:, :1] == device * doc_dev + (lane & (doc_dev - 1))
        signed = jnp.where(hit, -logits, logits)
        tail = jnp.exp(-jnp.abs(signed))
        losses = jnp.sum(jnp.maximum(signed, 0.0) + jnp.log1p(tail), axis=1, keepdims=True)
        chance = jnp.where(signed >= 0.0, 1.0, tail) / (1.0 + tail)
        grad = jnp.where(hit, -chance, chance)

        shape = (rings * packed, rings * recs)
        row, col = iota(shape, 0), iota(shape, 1)
        spread = selector(col == (row >> bits(packed)) * recs + (row & (recs - 1)))
        wide = dot(dot(spread, grad.astype(jnp.bfloat16)).astype(jnp.bfloat16), all_docs)
        chunk_at = (iota((rings * packed, lanes), 0) & (packed - 1)) >> bits(recs)
        picked = wide[:, :lanes]
        for chunk in range(1, chunks):
            span = slice(chunk * lanes, (chunk + 1) * lanes)
            picked = jnp.where(chunk_at == chunk, wide[:, span], picked)

        shape = (rings * 8, rings * recs)
        row, col = iota(shape, 0), iota(shape, 1)
        spread = selector(col == (row >> 3) * recs + (row & (recs - 1)))
        high = jnp.broadcast_to(losses.astype(jnp.bfloat16), (rings * recs, lanes))
        low = (losses - high.astype(jnp.float32)).astype(jnp.bfloat16)
        is_high = (iota((rings * 8, lanes), 0) & 7) < recs
        loss_rows = jnp.where(is_high, dot(spread, high), dot(spread, low))
        message = jnp.concatenate(
            [picked.reshape(rings, packed, lanes), loss_rows.reshape(rings, 8, lanes)], axis=1
        )
        grad_out[...] = message.astype(jnp.bfloat16)
        grad_move.send()
        grad_in[ring] = grad_out[ring]

        doc_part = dot(grad.T.astype(jnp.bfloat16), speech).astype(jnp.bfloat16)
        doc_out[...] = doc_part.reshape(team, doc_dev, width)
        doc_move.send()
        doc_in[member] = doc_out[member]

    def sum_grads():
        grad_move.receive()
        total = jnp.sum(grad_in[...].astype(jnp.float32), axis=0)
        total_out[...] = total
        total_move.send()
        total_in[column] = total

    def sum_docs():
        doc_move.receive()
        doc_grad_ref[...] = logit_scale * jnp.sum(doc_in[...].astype(jnp.float32), axis=0)

    def sum_totals():
        total_move.receive()
        total = jnp.sum(total_in[...], axis=0)
        for chunk in range(chunks):
            span = slice(chunk * lanes, (chunk + 1) * lanes)
            speech_grad_ref[:, span] = logit_scale * total[chunk * recs : (chunk + 1) * recs]
        loss_ref[...] = total[packed : packed + recs] + total[packed + recs : packed + 2 * recs]

    def drain():
        for move in (
            part_move,
            docs_move,
            speech_move,
            grad_move,
            doc_move,
            total_move,
        ):
            move.drain()

    enter()
    pool()
    meet_column()
    send_parts()
    fill_targets()
    open_ring()
    merge_parts()
    meet_ring()
    speech_move.send()
    send_docs()
    score()
    sum_grads()
    sum_docs()
    sum_totals()
    drain()


def finish(loss_ref, speech_grad_ref, doc_grad_ref, loss_out, speech_grad_out, doc_grad_out):
    speech_grad_out[...] = speech_grad_ref[...]
    doc_grad_out[...] = doc_grad_ref[...]
    shape = loss_ref.shape
    own = iota(shape, 0) == iota(shape, 1)
    loss_out[...] = jnp.sum(jnp.where(own, loss_ref[...], 0.0), axis=0)[: shape[0]]


def body(groups, columns, features, frame_counts, pool_query, w_proj, doc_embed, doc_index):
    recs, frames, channels = features.shape
    width = w_proj.shape[1]
    doc_dev = doc_embed.shape[0]
    rings = groups // team
    packed = width // lanes * recs
    vmem = pl.BlockSpec(memory_space=pltpu.VMEM)
    f32, bf16, i32 = jnp.float32, jnp.bfloat16, jnp.int32
    sems = pltpu.SemaphoreType.DMA
    loss, speech_grad, doc_grad = pl.pallas_call(
        functools.partial(kernel, rings, columns),
        out_shape=(
            jax.ShapeDtypeStruct((recs, lanes), f32),
            jax.ShapeDtypeStruct((recs, width), f32),
            jax.ShapeDtypeStruct((doc_dev, width), f32),
        ),
        in_specs=[pl.BlockSpec(memory_space=pltpu.MemorySpace.HBM)] * 6,
        out_specs=(vmem, vmem, vmem),
        scratch_shapes=[
            pltpu.SMEM(frame_counts.shape, i32),
            pltpu.SMEM(doc_index.shape, i32),
            pltpu.VMEM(features.shape, bf16),
            pltpu.VMEM(pool_query.shape, bf16),
            pltpu.VMEM(w_proj.shape, bf16),
            pltpu.VMEM((team, doc_dev, width), bf16),
            pltpu.VMEM((2 * packed, lanes), f32),
            pltpu.VMEM((columns, 2 * packed, lanes), f32),
            pltpu.VMEM((rings, packed, lanes), bf16),
            pltpu.VMEM((rings * recs, lanes), i32),
            pltpu.VMEM((rings, packed + 8, lanes), bf16),
            pltpu.VMEM((rings, packed + 8, lanes), bf16),
            pltpu.VMEM((packed + 8, lanes), f32),
            pltpu.VMEM((columns, packed + 8, lanes), f32),
            pltpu.VMEM((team, doc_dev, width), bf16),
            pltpu.VMEM((team, doc_dev, width), bf16),
            sems((6,)),
            sems((2, team)),
            sems((2, columns)),
            sems((2, rings)),
            sems((2, rings)),
            sems((2, columns)),
            sems((2, team)),
            pltpu.SemaphoreType.REGULAR,
            pltpu.SemaphoreType.REGULAR,
        ],
        compiler_params=pltpu.CompilerParams(
            collective_id=0, has_side_effects=True, vmem_limit_bytes=16 * 2**20
        ),
    )(
        *(
            pltpu.with_memory_space_constraint(array, pltpu.MemorySpace.HBM)
            for array in (frame_counts, doc_index, features, pool_query, w_proj, doc_embed)
        )
    )
    return pl.pallas_call(
        finish,
        out_shape=(
            jax.ShapeDtypeStruct((recs,), f32),
            jax.ShapeDtypeStruct((recs, width), f32),
            jax.ShapeDtypeStruct((doc_dev, width), f32),
        ),
        in_specs=[vmem] * 3,
        out_specs=(vmem, vmem, vmem),
        compiler_params=pltpu.CompilerParams(vmem_limit_bytes=16 * 2**20),
    )(loss, speech_grad, doc_grad)


def solution(mesh):
    placed = (P("grp", "tm", None), P("grp"), P(), P(), P(("grp", "tm"), None), P())
    return jax.shard_map(
        functools.partial(body, mesh.shape["grp"], mesh.shape["tm"]),
        mesh=mesh,
        in_specs=placed,
        out_specs=(P("grp"), P("grp", None), P(("grp", "tm"), None)),
        check_vma=False,
    )
```

```python
import functools
import math

import jax
import jax.numpy as jnp
from jax import lax
from jax.experimental import pallas as pl
from jax.experimental.pallas import tpu as pltpu
from jax.sharding import PartitionSpec as P

logit_scale = 10.0
logit_shift = -8.0
norm_eps = 1e-06
lowest = -1e30

team = 8
lanes = 128


def each(count, step):
    def run(index, carry):
        step(index)
        return carry

    lax.fori_loop(0, count, run, 0)


def bits(count):
    return count.bit_length() - 1


def iota(shape, axis):
    return lax.broadcasted_iota(jnp.int32, shape, axis)


def dot(a, b, contract_b=0):
    return lax.dot_general(
        a, b, (((1,), (contract_b,)), ((), ())), preferred_element_type=jnp.float32
    )


def selector(hit):
    return jnp.where(hit, 1.0, 0.0).astype(jnp.bfloat16)


def kernel(
    rings,
    columns,
    counts_ref,
    index_ref,
    feat_ref,
    query_ref,
    proj_ref,
    docs_ref,
    loss_ref,
    speech_grad_ref,
    doc_grad_ref,
    counts,
    index,
    feat,
    query,
    proj,
    docs,
    part_out,
    part_in,
    speech_in,
    target,
    grad_out,
    grad_in,
    total_out,
    total_in,
    doc_out,
    doc_in,
    load_sem,
    docs_sems,
    part_sems,
    speech_sems,
    grad_sems,
    total_sems,
    doc_sems,
    column_sem,
    ring_sem,
):
    recs, frames, channels = feat_ref.shape
    width = proj_ref.shape[1]
    heads = query_ref.shape[0]
    head_width = width // heads
    doc_dev = docs_ref.shape[0]
    chunks = width // lanes
    packed = chunks * recs

    group = lax.axis_index("grp")
    column = lax.axis_index("tm")
    ring = group >> bits(team)
    member = group & (team - 1)

    def ring_peer(step):
        off = (step + 1) >> 1
        other = (ring + rings // 2 + jnp.where((step & 1) == 1, -off, off)) & (rings - 1)
        return other, (other * team + member, column)

    def team_peer(step):
        other = member ^ (step + 1)
        return other, (ring * team + other, column)

    def column_peer(step):
        other = column ^ (step + 1)
        return other, (group, other)

    class Exchange:
        def __init__(self, count, own, peer, source, buffer, sems, same):
            self.count, self.own, self.peer = count, own, peer
            self.source, self.buffer, self.sems, self.same = source, buffer, sems, same

        def copy(self, step):
            other, device = self.peer(step)
            return pltpu.make_async_remote_copy(
                src_ref=self.source if self.same else self.source.at[other],
                dst_ref=self.buffer.at[self.own],
                send_sem=self.sems.at[0, other],
                recv_sem=self.sems.at[1, self.own],
                device_id=device,
                device_id_type=pl.DeviceIdType.MESH,
            )

        def send(self):
            each(self.count - 1, lambda step: self.copy(step).start())

        def receive(self):
            def arrival(step):
                block = self.buffer.at[self.own ^ (step + 1)]
                pltpu.make_async_copy(
                    block, block, self.sems.at[1, self.own ^ (step + 1)]
                ).wait()

            each(self.count - 1, arrival)

        def drain(self):
            each(self.count - 1, lambda step: self.copy(step).wait_send())

    along_ring = functools.partial(Exchange, rings, ring, ring_peer)
    in_team = functools.partial(Exchange, team, member, team_peer)
    in_column = functools.partial(Exchange, columns, column, column_peer)
    docs_move = in_team(docs.at[member], docs, docs_sems, True)
    part_move = in_column(part_out, part_in, part_sems, True)
    speech_move = along_ring(speech_in.at[ring], speech_in, speech_sems, True)
    grad_move = along_ring(grad_out, grad_in, grad_sems, False)
    total_move = in_column(total_out, total_in, total_sems, True)
    doc_move = in_team(doc_out, doc_in, doc_sems, False)

    sources = [(query_ref, query), (counts_ref, counts)]
    sources += [(feat_ref.at[rec], feat.at[rec]) for rec in range(recs)]
    sources += [(proj_ref, proj), (docs_ref, docs.at[member]), (index_ref, index)]
    loads = [
        pltpu.make_async_copy(source, buffer, load_sem.at[number])
        for number, (source, buffer) in enumerate(sources)
    ]
    proj_load, docs_load, index_load = loads[-3:]
    barrier = pltpu.get_barrier_semaphore()

    def greet(device):
        pl.semaphore_signal(
            barrier, inc=1, device_id=device, device_id_type=pl.DeviceIdType.MESH
        )

    def enter():
        for load in loads:
            load.start()
        even = column - (column & 1)
        each(rings - 1, lambda step: greet((ring_peer(step)[1][0], even)))
        each(team - 1, lambda step: greet((team_peer(step)[1][0], even)))

        def greet_odd(step):
            @pl.when(step * 2 + 1 != column)
            def _():
                greet((group, step * 2 + 1))

        each(columns // 2, greet_odd)

    def pool():
        for load in loads[:-3]:
            load.wait()
        every = feat[...].reshape(recs * frames, channels)
        all_scores = dot(query[...], every, 1) / math.sqrt(channels)
        position = column * frames + iota((heads, frames), 1)
        lane_head = iota((heads, width), 1) >> bits(head_width)
        own_head = lane_head == iota((heads, width), 0)
        means, levels = [], []
        for rec in range(recs):
            scores = all_scores[:, rec * frames : (rec + 1) * frames]
            valid = position < counts[rec]
            masked = jnp.where(valid, scores, lowest)
            peak = jnp.max(masked, axis=1, keepdims=True)
            weights = jnp.where(valid, jnp.exp(masked - peak), 0.0)
            total = jnp.sum(weights, axis=1, keepdims=True)
            some = total > 0.0
            safe = jnp.where(some, total, 1.0)
            means.append(dot(weights.astype(jnp.bfloat16), feat[rec]) / safe)
            levels.append(jnp.where(some, peak + jnp.log(safe), lowest))
        means = jnp.concatenate(means, axis=0)
        high = means.astype(jnp.bfloat16)
        low = (means - high.astype(jnp.float32)).astype(jnp.bfloat16)
        proj_load.wait()
        projected = dot(jnp.concatenate([high, low], axis=0), proj[...])
        projected = projected[: recs * heads] + projected[recs * heads :]
        for rec in range(recs):
            own = projected[rec * heads : (rec + 1) * heads]
            row = jnp.sum(jnp.where(own_head, own, 0.0), axis=0, keepdims=True)
            level = jnp.sum(jnp.where(own_head, levels[rec], 0.0), axis=0, keepdims=True)
            for chunk in range(chunks):
                at = chunk * recs + rec
                span = slice(chunk * lanes, (chunk + 1) * lanes)
                part_out[at : at + 1, :] = row[:, span]
                part_out[packed + at : packed + at + 1, :] = level[:, span]

    is_odd = (column & 1) == 1

    def tell_partner(sem):
        pl.semaphore_signal(
            sem, inc=1, device_id=(group, column ^ 1), device_id_type=pl.DeviceIdType.MESH
        )

    def meet_column():
        @pl.when(is_odd)
        def _():
            pl.semaphore_wait(barrier, columns - 1)
            tell_partner(column_sem)

        @pl.when(jnp.logical_not(is_odd))
        def _():
            pl.semaphore_wait(column_sem, 1)

    def open_ring():
        @pl.when(jnp.logical_not(is_odd))
        def _():
            pl.semaphore_wait(barrier, 2 * (rings - 1 + team - 1))
            tell_partner(ring_sem)

    def meet_ring():
        @pl.when(is_odd)
        def _():
            pl.semaphore_wait(ring_sem, 1)

    def send_parts():
        part_move.send()
        part_in[column] = part_out[...]

    def send_docs():
        docs_load.wait()
        docs_move.send()

    def fill_targets():
        index_load.wait()
        row = iota((8, lanes), 0)

        def fill(block):
            value = jnp.zeros((8, lanes), jnp.int32)
            for j in range(8):
                place = block * (8 // recs) + j // recs
                number = (place * team + member) * recs + j % recs
                value = jnp.where(row == j, index[number], value)
            target[pl.ds(pl.multiple_of(block * 8, 8), 8), :] = value

        each(rings * recs // 8, fill)

    def merge_parts():
        part_move.receive()
        parts = part_in[...]
        levels = parts[:, packed:, :]
        shares = jnp.exp(levels - jnp.max(levels, axis=0, keepdims=True))
        mean = jnp.sum(shares * parts[:, :packed, :], axis=0) / jnp.sum(shares, axis=0)
        squares = jnp.sum(mean * mean, axis=1, keepdims=True)
        rec_at = iota((packed, 1), 0) & (recs - 1)
        sums = jnp.zeros((packed, 1), jnp.float32)
        for rec in range(recs):
            mine = rec_at == rec
            sums = jnp.where(
                mine, jnp.sum(jnp.where(mine, squares, 0.0), axis=0, keepdims=True), sums
            )
        speech_in[ring] = (mean * lax.rsqrt(sums + norm_eps)).astype(jnp.bfloat16)

    def score():
        docs_move.receive()
        speech_move.receive()
        pieces = speech_in[...].reshape(rings * packed, lanes)
        shape = (rings * recs, rings * packed)
        row, col = iota(shape, 0), iota(shape, 1)
        base = (row >> bits(recs)) * packed + (row & (recs - 1))
        whole = [
            dot(selector(col == base + chunk * recs), pieces).astype(jnp.bfloat16)
            for chunk in range(chunks)
        ]
        speech = jnp.concatenate(whole, axis=1)
        all_docs = docs[...].reshape(team * doc_dev, width)
        logits = logit_scale * dot(speech, all_docs, 1) + logit_shift
        lane = iota((1, team * doc_dev), 1)
        device = (ring * team + (lane >> bits(doc_dev))) * columns + column
        hit = target[:, :1] == device * doc_dev + (lane & (doc_dev - 1))
        signed = jnp.where(hit, -logits, logits)
        tail = jnp.exp(-jnp.abs(signed))
        losses = jnp.sum(jnp.maximum(signed, 0.0) + jnp.log1p(tail), axis=1, keepdims=True)
        chance = jnp.where(signed >= 0.0, 1.0, tail) / (1.0 + tail)
        grad = jnp.where(hit, -chance, chance)

        shape = (rings * packed, rings * recs)
        row, col = iota(shape, 0), iota(shape, 1)
        spread = selector(col == (row >> bits(packed)) * recs + (row & (recs - 1)))
        wide = dot(dot(spread, grad.astype(jnp.bfloat16)).astype(jnp.bfloat16), all_docs)
        chunk_at = (iota((rings * packed, lanes), 0) & (packed - 1)) >> bits(recs)
        picked = wide[:, :lanes]
        for chunk in range(1, chunks):
            span = slice(chunk * lanes, (chunk + 1) * lanes)
            picked = jnp.where(chunk_at == chunk, wide[:, span], picked)

        shape = (rings * 8, rings * recs)
        row, col = iota(shape, 0), iota(shape, 1)
        spread = selector(col == (row >> 3) * recs + (row & (recs - 1)))
        high = jnp.broadcast_to(losses.astype(jnp.bfloat16), (rings * recs, lanes))
        low = (losses - high.astype(jnp.float32)).astype(jnp.bfloat16)
        is_high = (iota((rings * 8, lanes), 0) & 7) < recs
        loss_rows = jnp.where(is_high, dot(spread, high), dot(spread, low))
        message = jnp.concatenate(
            [picked.reshape(rings, packed, lanes), loss_rows.reshape(rings, 8, lanes)], axis=1
        )
        grad_out[...] = message.astype(jnp.bfloat16)
        grad_move.send()
        grad_in[ring] = grad_out[ring]

        doc_part = dot(grad.T.astype(jnp.bfloat16), speech).astype(jnp.bfloat16)
        doc_out[...] = doc_part.reshape(team, doc_dev, width)
        doc_move.send()
        doc_in[member] = doc_out[member]

    def sum_grads():
        grad_move.receive()
        total = jnp.sum(grad_in[...].astype(jnp.float32), axis=0)
        total_out[...] = total
        total_move.send()
        total_in[column] = total

    def sum_docs():
        doc_move.receive()
        doc_grad_ref[...] = logit_scale * jnp.sum(doc_in[...].astype(jnp.float32), axis=0)

    def sum_totals():
        total_move.receive()
        total = jnp.sum(total_in[...], axis=0)
        for chunk in range(chunks):
            span = slice(chunk * lanes, (chunk + 1) * lanes)
            speech_grad_ref[:, span] = logit_scale * total[chunk * recs : (chunk + 1) * recs]
        loss_ref[...] = total[packed : packed + recs] + total[packed + recs : packed + 2 * recs]

    def drain():
        for move in (
            part_move,
            docs_move,
            speech_move,
            grad_move,
            doc_move,
            total_move,
        ):
            move.drain()

    enter()
    pool()
    meet_column()
    send_parts()
    fill_targets()
    open_ring()
    merge_parts()
    meet_ring()
    speech_move.send()
    send_docs()
    score()
    sum_grads()
    sum_docs()
    sum_totals()
    drain()


def finish(loss_ref, speech_grad_ref, doc_grad_ref, loss_out, speech_grad_out, doc_grad_out):
    speech_grad_out[...] = speech_grad_ref[...]
    doc_grad_out[...] = doc_grad_ref[...]
    shape = loss_ref.shape
    own = iota(shape, 0) == iota(shape, 1)
    loss_out[...] = jnp.sum(jnp.where(own, loss_ref[...], 0.0), axis=0)[: shape[0]]


def body(groups, columns, features, frame_counts, pool_query, w_proj, doc_embed, doc_index):
    recs, frames, channels = features.shape
    width = w_proj.shape[1]
    doc_dev = doc_embed.shape[0]
    rings = groups // team
    packed = width // lanes * recs
    vmem = pl.BlockSpec(memory_space=pltpu.VMEM)
    f32, bf16, i32 = jnp.float32, jnp.bfloat16, jnp.int32
    sems = pltpu.SemaphoreType.DMA
    loss, speech_grad, doc_grad = pl.pallas_call(
        functools.partial(kernel, rings, columns),
        out_shape=(
            jax.ShapeDtypeStruct((recs, lanes), f32),
            jax.ShapeDtypeStruct((recs, width), f32),
            jax.ShapeDtypeStruct((doc_dev, width), f32),
        ),
        in_specs=[pl.BlockSpec(memory_space=pltpu.MemorySpace.HBM)] * 6,
        out_specs=(vmem, vmem, vmem),
        scratch_shapes=[
            pltpu.SMEM(frame_counts.shape, i32),
            pltpu.SMEM(doc_index.shape, i32),
            pltpu.VMEM(features.shape, bf16),
            pltpu.VMEM(pool_query.shape, bf16),
            pltpu.VMEM(w_proj.shape, bf16),
            pltpu.VMEM((team, doc_dev, width), bf16),
            pltpu.VMEM((2 * packed, lanes), f32),
            pltpu.VMEM((columns, 2 * packed, lanes), f32),
            pltpu.VMEM((rings, packed, lanes), bf16),
            pltpu.VMEM((rings * recs, lanes), i32),
            pltpu.VMEM((rings, packed + 8, lanes), bf16),
            pltpu.VMEM((rings, packed + 8, lanes), bf16),
            pltpu.VMEM((packed + 8, lanes), f32),
            pltpu.VMEM((columns, packed + 8, lanes), f32),
            pltpu.VMEM((team, doc_dev, width), bf16),
            pltpu.VMEM((team, doc_dev, width), bf16),
            sems((recs + 5,)),
            sems((2, team)),
            sems((2, columns)),
            sems((2, rings)),
            sems((2, rings)),
            sems((2, columns)),
            sems((2, team)),
            pltpu.SemaphoreType.REGULAR,
            pltpu.SemaphoreType.REGULAR,
        ],
        compiler_params=pltpu.CompilerParams(
            collective_id=0, has_side_effects=True, vmem_limit_bytes=16 * 2**20
        ),
    )(
        *(
            pltpu.with_memory_space_constraint(array, pltpu.MemorySpace.HBM)
            for array in (frame_counts, doc_index, features, pool_query, w_proj, doc_embed)
        )
    )
    return pl.pallas_call(
        finish,
        out_shape=(
            jax.ShapeDtypeStruct((recs,), f32),
            jax.ShapeDtypeStruct((recs, width), f32),
            jax.ShapeDtypeStruct((doc_dev, width), f32),
        ),
        in_specs=[vmem] * 3,
        out_specs=(vmem, vmem, vmem),
        compiler_params=pltpu.CompilerParams(vmem_limit_bytes=16 * 2**20),
    )(loss, speech_grad, doc_grad)


def solution(mesh):
    placed = (P("grp", "tm", None), P("grp"), P(), P(), P(("grp", "tm"), None), P())
    return jax.shard_map(
        functools.partial(body, mesh.shape["grp"], mesh.shape["tm"]),
        mesh=mesh,
        in_specs=placed,
        out_specs=(P("grp"), P("grp", None), P(("grp", "tm"), None)),
        check_vma=False,
    )
```
